32 devices in a mesh: groups: 2 (over y), tensor: 4 (over z), dp: 4 (over x, core).
Axes of the slice: x: 2, y: 2, z: 4, core: 2. Of those that a mesh axis runs over, the one named last changes fastest.
Arguments:
- out_grad: bfloat16 [4, 1280, 4096], P('dp', ('groups', 'tensor')), parts along dimension 1, may hold values from -6 to 6
- gate_pre: bfloat16 [4, 1280, 14336], P('dp', 'groups', 'tensor'), parts along dimension 1, may hold values from -8 to 8
- up_pre: bfloat16 [4, 1280, 14336], P('dp', 'groups', 'tensor'), parts along dimension 1, may hold values from -6 to 6
- down_weight: bfloat16 [14336, 4096], P('tensor'), may hold values from -0.046875 to 0.046875
Outputs:
- gate_grad: bfloat16 [4, 1280, 14336], P('dp', 'groups', 'tensor'), parts along dimension 1
- up_grad: bfloat16 [4, 1280, 14336], P('dp', 'groups', 'tensor'), parts along dimension 1
- down_grad: bfloat16 [28672, 4096], P(('groups', 'tensor'), 'dp'), parts along dimension 0
The draws below stay inside these ranges and needn't reach their ends.
There are 2 independent parts, one for each index of `groups`. The reference program is written for one: setup_inputs(seed, part) draws one part's arguments, and reference() takes and returns one part's arrays. A program takes and returns all parts, laid end to end along the dimension named above; an argument that names none is the same for every part. Nothing has to cross between parts.
All inputs are finite; a program needn't handle non-finite values.
Results may differ from the reference program's by a relative error of at most 0.014.
Values may be sent and summed in bfloat16 or wider, within the bound.
A program may use at most 128 MiB of HBM per device.

```python
import math
import jax
import jax.numpy as jnp
from jax import lax

D = 4096
FF = 14336
TOK_GROUP = 640
DATA = 4
TOKENS = 2560


def block_scale(rng, extent, pieces, low, high):
    gain, own = 1.0, jax.random.fold_in(rng, 6)
    for position, parts in pieces:
        draws = jnp.exp(jax.random.uniform(jax.random.fold_in(own, position), (parts,), jnp.float32, low / len(pieces), high / len(pieces)))
        gain = gain * jnp.repeat(draws, extent[position] // parts).reshape([-1 if axis == position else 1 for axis in range(len(extent))])
    return gain


def centred(rng, extent, width, reach, pieces=(), kind=jnp.bfloat16):
    level = block_scale(rng, extent, pieces, -0.22, 0.18) if pieces else 1.0
    drawn = jax.random.normal(rng, extent, jnp.float32) * width * level
    return jnp.minimum(jnp.maximum(drawn, -reach), reach).astype(kind)


def setup_inputs(seed: int = 0, part: int = 0) -> dict:
    arg_keys = jax.random.split(jax.random.key(seed), 5)
    own_keys = jax.random.split(jax.random.fold_in(arg_keys[4], part), 5)
    return {
        "out_grad": centred(own_keys[0], (DATA, TOK_GROUP, D), 1.0, 6.0, ((0, 4), (1, 4))),
        "gate_pre": centred(own_keys[1], (DATA, TOK_GROUP, FF), 1.5, 8.0, ((0, 4), (2, 4))),
        "up_pre": centred(own_keys[2], (DATA, TOK_GROUP, FF), 1.0, 6.0, ((0, 4), (2, 4))),
        "down_weight": centred(arg_keys[3], (FF, D), FF ** -0.5, 0.046875, ((0, 4),)),
    }


def reference(out_grad, gate_pre, up_pre, down_weight):
    gate = gate_pre.astype(jnp.float32)
    up = up_pre.astype(jnp.float32)
    sig = jax.nn.sigmoid(gate)
    act = gate * sig
    hidden = (act * up).astype(jnp.bfloat16)
    scale = 1.0 / math.sqrt(TOKENS)
    indices = jnp.arange(DATA)

    def group_term(total, index):
        term = jnp.dot(hidden[index].T, out_grad[index], preferred_element_type=jnp.float32) * scale
        rounded = lax.optimization_barrier(term.astype(jnp.bfloat16))
        return (total + rounded.astype(jnp.float32), None)
    total, _ = lax.scan(group_term, jnp.zeros((FF, D), jnp.float32), indices)

    def group_grad(index):
        return jnp.dot(out_grad[index], down_weight.T, preferred_element_type=jnp.float32)
    hidden_grad = lax.map(group_grad, indices)
    gate_grad = (hidden_grad * up * sig * (1.0 + gate * (1.0 - sig))).astype(jnp.bfloat16)
    up_grad = (hidden_grad * act).astype(jnp.bfloat16)
    return (gate_grad, up_grad, total.astype(jnp.bfloat16))
```

```python
import math

import jax
import jax.numpy as jnp
from jax import lax
from jax.sharding import PartitionSpec as P


def on_device(out_grad, gate_pre, up_pre, down_weight):
    gate = gate_pre[0].astype(jnp.float32)
    up = up_pre[0].astype(jnp.float32)
    sig = jax.nn.sigmoid(gate)
    act = gate * sig
    hidden = (act * up).astype(jnp.bfloat16)
    scale = 1.0 / math.sqrt(hidden.shape[0] * lax.axis_size("dp"))
    hidden_all = lax.all_gather(hidden, "dp", axis=0, tiled=True)
    block = lax.all_gather(out_grad, "tensor", axis=1, tiled=True)[0]
    columns = lax.all_to_all(block, "dp", split_axis=1, concat_axis=0, tiled=True)
    hidden_grad = lax.dot_general(
        block, down_weight, (((1,), (1,)), ((), ())), preferred_element_type=jnp.float32
    )
    gate_grad = (hidden_grad * up * sig * (1.0 + gate * (1.0 - sig))).astype(jnp.bfloat16)
    up_grad = (hidden_grad * act).astype(jnp.bfloat16)
    total = jnp.einsum("tf,td->fd", hidden_all, columns, preferred_element_type=jnp.float32)
    down_grad = (total * scale).astype(jnp.bfloat16)
    return (gate_grad[None], up_grad[None], down_grad)


def solution(mesh):
    return jax.shard_map(
        on_device,
        mesh=mesh,
        in_specs=(
            P("dp", ("groups", "tensor"), None),
            P("dp", "groups", "tensor"),
            P("dp", "groups", "tensor"),
            P("tensor", None),
        ),
        out_specs=(
            P("dp", "groups", "tensor"),
            P("dp", "groups", "tensor"),
            P(("groups", "tensor"), "dp"),
        ),
        check_vma=False,
    )
```

```python
import functools
import math

import jax
import jax.numpy as jnp
from jax import lax
from jax.experimental import pallas as pl
from jax.experimental.pallas import tpu as pltpu
from jax.sharding import PartitionSpec as P

A_PIECES = 4
B_PIECES = 2
H_PIECES = 8
MESH = pl.DeviceIdType.MESH


def exchange(
    nt, nx, tile,
    og, gate, up, weight,
    hid, cols, gate_grad, up_grad,
    og_v, xb_v, hid_v,
    own_sem, a_recv, a_up, a_dn, x_send, x_recv, b_recv, b_up, b_dn,
    hx_send, hp_send, hl_sem, h_recv, hf_send, c_local, c_send, c_recv,
):
    t = lax.axis_index("tensor")
    d = lax.axis_index("dp")
    x, c = d // 2, d % 2
    mate = x * 2 + (1 - c)
    rows, width = og.shape
    tokens, hidden_width = gate.shape
    chip_cols = width // nx
    dev_cols = width // (2 * nx)
    a_cols = width // A_PIECES
    b_cols = chip_cols // B_PIECES
    h_rows = tokens // H_PIECES
    has_up, has_dn = t < nt - 1, t > 0

    def span(i, size):
        return pl.ds(pl.multiple_of(i * size, size), size)

    def remote(src, dst, send, recv, **where):
        return pltpu.make_async_remote_copy(
            src_ref=src, dst_ref=dst, send_sem=send, recv_sem=recv,
            device_id=where, device_id_type=MESH,
        )

    def other(j):
        return (x + j) % nx

    barrier = pltpu.get_barrier_semaphore()

    @pl.when(has_up)
    def _():
        pl.semaphore_signal(barrier, 1, device_id={"tensor": t + 1}, device_id_type=MESH)

    @pl.when(has_dn)
    def _():
        pl.semaphore_signal(barrier, 1, device_id={"tensor": t - 1}, device_id_type=MESH)

    pl.semaphore_signal(barrier, 1, device_id={"dp": mate}, device_id_type=MESH)
    for j in range(1, nx):
        pl.semaphore_signal(barrier, 1, device_id={"dp": other(j) * 2 + c}, device_id_type=MESH)
    inner = jnp.logical_and(has_up, has_dn)

    @pl.when(inner)
    def _():
        pl.semaphore_wait(barrier, nx + 2)

    @pl.when(jnp.logical_not(inner))
    def _():
        pl.semaphore_wait(barrier, nx + 1)

    def a_copy(src, o, p, to, sems):
        return remote(src, og_v.at[o, :, span(p, a_cols)], sems.at[o, p], a_recv.at[o, p], tensor=to)

    def a_fwd(o, p, to, sems):
        return a_copy(og_v.at[o, :, span(p, a_cols)], o, p, to, sems)

    def b_fwd(o, xs, p, to, sems):
        ref = xb_v.at[xs, o, :, span(p, b_cols)]
        return remote(ref, ref, sems.at[o, xs, p], b_recv.at[o, xs, p], tensor=to)

    def x_copy(j):
        xo = other(j)
        return remote(
            og.at[:, span(xo, chip_cols)], xb_v.at[x, t], x_send.at[j], x_recv.at[x], dp=xo * 2 + c
        )

    own = pltpu.make_async_copy(og, og_v.at[t], own_sem)
    own.start()
    for p in range(A_PIECES):
        @pl.when(has_up)
        def _():
            a_copy(og.at[:, span(p, a_cols)], t, p, t + 1, a_up).start()

        @pl.when(has_dn)
        def _():
            a_copy(og.at[:, span(p, a_cols)], t, p, t - 1, a_dn).start()
    for j in range(1, nx):
        x_copy(j).start()

    def h_to(src, owner, i, sem, to):
        return remote(src, hid.at[owner, span(i, h_rows)], sem, h_recv.at[owner, i], dp=to)

    def h_own(i):
        src = hid_v.at[span(i, h_rows)]
        out = [h_to(src, d, i, hx_send.at[j, i], other(j) * 2 + c) for j in range(1, nx)]
        out.append(h_to(src, d, i, hp_send.at[i], mate))
        out.append(pltpu.make_async_copy(src, hid.at[d, span(i, h_rows)], hl_sem.at[i]))
        return out

    def h_fwd(j, i):
        owner = other(j) * 2 + c
        return h_to(hid.at[owner, span(i, h_rows)], owner, i, hf_send.at[j, i], mate)

    def hidden_step(gate_t, up_t):
        i = pl.program_id(0)
        g = gate_t[...].astype(jnp.float32)
        u = up_t[...].astype(jnp.float32)
        hid_v[span(i, h_rows), :] = (g * jax.nn.sigmoid(g) * u).astype(jnp.bfloat16)
        for copy in h_own(i):
            copy.start()

    row_spec = pl.BlockSpec((h_rows, hidden_width), lambda i: (i, 0))
    pltpu.emit_pipeline(hidden_step, grid=(H_PIECES,), in_specs=[row_spec, row_spec])(gate, up)

    @pl.loop(0, (nt - 1) * A_PIECES)
    def _(e):
        k, p = e // A_PIECES + 1, e % A_PIECES

        @pl.when(t - k >= 0)
        def _():
            a_fwd(t - k, p, t + 1, a_up).wait_recv()

            @pl.when(has_up)
            def _():
                a_fwd(t - k, p, t + 1, a_up).start()

        @pl.when(t + k < nt)
        def _():
            a_fwd(t + k, p, t - 1, a_dn).wait_recv()

            @pl.when(has_dn)
            def _():
                a_fwd(t + k, p, t - 1, a_dn).start()

    own.wait()
    for j in range(1, nx):
        xs = other(j)
        remote(xb_v.at[xs, t], xb_v.at[xs, t], x_send.at[j], x_recv.at[xs], dp=mate).wait_recv()
        for p in range(B_PIECES):
            @pl.when(has_up)
            def _():
                b_fwd(t, xs, p, t + 1, b_up).start()

            @pl.when(has_dn)
            def _():
                b_fwd(t, xs, p, t - 1, b_dn).start()

    def c_copies(owner, xs, ref, mine, theirs):
        return (
            pltpu.make_async_copy(ref.at[:, :, span(mine, dev_cols)], cols.at[owner], c_local.at[xs]),
            remote(ref.at[:, :, span(theirs, dev_cols)], cols.at[owner], c_send.at[xs], c_recv.at[owner], dp=mate),
        )

    for copy in c_copies(d, x, og_v, d, mate):
        copy.start()

    b_events = (nt - 1) * (nx - 1) * B_PIECES
    h_events = (nx - 1) * H_PIECES
    steps = hidden_width // tile
    per_step = -(-(b_events + h_events) // steps)

    def event(e):
        @pl.when(e < b_events)
        def _():
            k = e // ((nx - 1) * B_PIECES) + 1
            q = e % ((nx - 1) * B_PIECES)
            xs, p = other(q // B_PIECES + 1), q % B_PIECES

            @pl.when(t - k >= 0)
            def _():
                b_fwd(t - k, xs, p, t + 1, b_up).wait_recv()

                @pl.when(has_up)
                def _():
                    b_fwd(t - k, xs, p, t + 1, b_up).start()

            @pl.when(t + k < nt)
            def _():
                b_fwd(t + k, xs, p, t - 1, b_dn).wait_recv()

                @pl.when(has_dn)
                def _():
                    b_fwd(t + k, xs, p, t - 1, b_dn).start()

        @pl.when(jnp.logical_and(e >= b_events, e < b_events + h_events))
        def _():
            f = e - b_events
            h_fwd(f % (nx - 1) + 1, f // (nx - 1)).wait_recv()
            h_fwd(f % (nx - 1) + 1, f // (nx - 1)).start()

    def grad_step(w_t, gate_t, up_t, gg_t, ug_t):
        i = pl.program_id(0)
        block = og_v[...].reshape(nt * rows, width)
        grad = lax.dot_general(
            block, w_t[...], (((1,), (1,)), ((), ())), preferred_element_type=jnp.float32
        )
        g = gate_t[...].astype(jnp.float32)
        u = up_t[...].astype(jnp.float32)
        sig = jax.nn.sigmoid(g)
        gg_t[...] = (grad * u * sig * (1.0 + g * (1.0 - sig))).astype(jnp.bfloat16)
        ug_t[...] = (grad * (g * sig)).astype(jnp.bfloat16)
        for s in range(per_step):
            event(i * per_step + s)

    tile_spec = pl.BlockSpec((tokens, tile), lambda i: (0, i))
    pltpu.emit_pipeline(
        grad_step,
        grid=(steps,),
        in_specs=[pl.BlockSpec((tile, width), lambda i: (i, 0)), tile_spec, tile_spec],
        out_specs=[tile_spec, tile_spec],
    )(weight, gate, up, gate_grad, up_grad)

    for j in range(1, nx):
        xs = other(j)
        for copy in c_copies(xs * 2 + c, xs, xb_v.at[xs], c, 1 - c):
            copy.start()

    for j in range(nx):
        xs = other(j)
        local, sent = c_copies(xs * 2 + c, xs, xb_v.at[xs], c, 1 - c)
        local.wait()
        sent.wait_send()
        c_copies(xs * 2 + 1 - c, xs, xb_v.at[xs], c, 1 - c)[1].wait_recv()
    for j in range(1, nx):
        x_copy(j).wait_send()

    @pl.loop(0, H_PIECES)
    def _(i):
        *sent, local = h_own(i)
        for copy in sent:
            copy.wait_send()
        local.wait()
        for j in range(nx):
            owner = other(j) * 2 + 1 - c
            h_to(hid_v.at[span(i, h_rows)], owner, i, hp_send.at[i], mate).wait_recv()
        for j in range(1, nx):
            h_fwd(j, i).wait_send()

    @pl.loop(0, nt)
    def _(o):
        @pl.when(jnp.logical_and(has_up, o <= t))
        def _():
            for p in range(A_PIECES):
                a_fwd(o, p, t + 1, a_up).wait_send()
            for j in range(1, nx):
                for p in range(B_PIECES):
                    b_fwd(o, other(j), p, t + 1, b_up).wait_send()

        @pl.when(jnp.logical_and(has_dn, o >= t))
        def _():
            for p in range(A_PIECES):
                a_fwd(o, p, t - 1, a_dn).wait_send()
            for j in range(1, nx):
                for p in range(B_PIECES):
                    b_fwd(o, other(j), p, t - 1, b_dn).wait_send()


def on_device(out_grad, gate_pre, up_pre, down_weight):
    nt, dp = lax.axis_size("tensor"), lax.axis_size("dp")
    nx = dp // 2
    _, rows, width = out_grad.shape
    _, tokens, hidden_width = gate_pre.shape
    tile = 256 if hidden_width % 256 == 0 else 128
    bf16 = jnp.bfloat16
    dma = pltpu.SemaphoreType.DMA
    any_spec = pl.BlockSpec(memory_space=pl.ANY)
    hid, cols, gate_grad, up_grad = pl.pallas_call(
        functools.partial(exchange, nt, nx, tile),
        out_shape=(
            jax.ShapeDtypeStruct((dp, tokens, hidden_width), bf16),
            jax.ShapeDtypeStruct((dp, nt, rows, width // dp), bf16),
            jax.ShapeDtypeStruct((tokens, hidden_width), bf16),
            jax.ShapeDtypeStruct((tokens, hidden_width), bf16),
        ),
        in_specs=[any_spec] * 4,
        out_specs=[any_spec] * 4,
        scratch_shapes=[
            pltpu.VMEM((nt, rows, width), bf16),
            pltpu.VMEM((nx, nt, rows, width // nx), bf16),
            pltpu.VMEM((tokens, hidden_width), bf16),
            dma,
            dma((nt, A_PIECES)),
            dma((nt, A_PIECES)),
            dma((nt, A_PIECES)),
            dma((nx,)),
            dma((nx,)),
            dma((nt, nx, B_PIECES)),
            dma((nt, nx, B_PIECES)),
            dma((nt, nx, B_PIECES)),
            dma((nx, H_PIECES)),
            dma((H_PIECES,)),
            dma((H_PIECES,)),
            dma((dp, H_PIECES)),
            dma((nx, H_PIECES)),
            dma((nx,)),
            dma((nx,)),
            dma((dp,)),
        ],
        compiler_params=pltpu.CompilerParams(
            collective_id=0, has_side_effects=True, vmem_limit_bytes=56 * 2**20
        ),
    )(out_grad[0], gate_pre[0], up_pre[0], down_weight)
    scale = 1.0 / math.sqrt(tokens * dp)
    total = jnp.einsum(
        "tf,td->fd",
        hid.reshape(dp * tokens, hidden_width),
        cols.reshape(dp * tokens, width // dp),
        preferred_element_type=jnp.float32,
    )
    down_grad = (total * scale).astype(bf16)
    return (gate_grad[None], up_grad[None], down_grad)


def solution(mesh):
    return jax.shard_map(
        on_device,
        mesh=mesh,
        in_specs=(
            P("dp", ("groups", "tensor"), None),
            P("dp", "groups", "tensor"),
            P("dp", "groups", "tensor"),
            P("tensor", None),
        ),
        out_specs=(
            P("dp", "groups", "tensor"),
            P("dp", "groups", "tensor"),
            P(("groups", "tensor"), "dp"),
        ),
        check_vma=False,
    )
```

```python
import functools
import math

import jax
import jax.numpy as jnp
from jax import lax
from jax.experimental import pallas as pl
from jax.experimental.pallas import tpu as pltpu
from jax.sharding import PartitionSpec as P

A_PIECES = 4
B_PIECES = 2
H_PIECES = 8
MESH = pl.DeviceIdType.MESH


def exchange(
    nt, nx, tile,
    og, gate, up, weight,
    hid_own, hid_far, cols_own, cols_far, partial, gate_grad, up_grad,
    og_v, xb_v, hid_v,
    own_sem, a_recv, a_up, a_dn, x_send, x_recv, b_recv, b_up, b_dn,
    hx_send, hp_send, hl_sem, ho_recv, hf_recv, hf_send,
    c_local, c_send, c_recv, f_local, f_send, f_recv,
):
    t = lax.axis_index("tensor")
    d = lax.axis_index("dp")
    x, c = d // 2, d % 2
    mate = x * 2 + (1 - c)
    rows, width = og.shape
    tokens, hidden_width = gate.shape
    chip_cols = width // nx
    dev_cols = width // (2 * nx)
    a_cols = width // A_PIECES
    b_cols = chip_cols // B_PIECES
    h_rows = tokens // H_PIECES
    has_up, has_dn = t < nt - 1, t > 0

    def span(i, size):
        return pl.ds(pl.multiple_of(i * size, size), size)

    def remote(src, dst, send, recv, **where):
        return pltpu.make_async_remote_copy(
            src_ref=src, dst_ref=dst, send_sem=send, recv_sem=recv,
            device_id=where, device_id_type=MESH,
        )

    def other(j):
        return (x + j) % nx

    barrier = pltpu.get_barrier_semaphore()

    @pl.when(has_up)
    def _():
        pl.semaphore_signal(barrier, 1, device_id={"tensor": t + 1}, device_id_type=MESH)

    @pl.when(has_dn)
    def _():
        pl.semaphore_signal(barrier, 1, device_id={"tensor": t - 1}, device_id_type=MESH)

    pl.semaphore_signal(barrier, 1, device_id={"dp": mate}, device_id_type=MESH)
    for j in range(1, nx):
        pl.semaphore_signal(barrier, 1, device_id={"dp": other(j) * 2 + c}, device_id_type=MESH)
    inner = jnp.logical_and(has_up, has_dn)

    @pl.when(inner)
    def _():
        pl.semaphore_wait(barrier, nx + 2)

    @pl.when(jnp.logical_not(inner))
    def _():
        pl.semaphore_wait(barrier, nx + 1)

    def a_copy(src, o, p, to, sems):
        return remote(src, og_v.at[o, :, span(p, a_cols)], sems.at[o, p], a_recv.at[o, p], tensor=to)

    def a_fwd(o, p, to, sems):
        return a_copy(og_v.at[o, :, span(p, a_cols)], o, p, to, sems)

    def b_fwd(o, xs, p, to, sems):
        ref = xb_v.at[xs, o, :, span(p, b_cols)]
        return remote(ref, ref, sems.at[o, xs, p], b_recv.at[o, xs, p], tensor=to)

    def x_copy(j):
        xo = other(j)
        return remote(
            og.at[:, span(xo, chip_cols)], xb_v.at[x, t], x_send.at[j], x_recv.at[x], dp=xo * 2 + c
        )

    own = pltpu.make_async_copy(og, og_v.at[t], own_sem)
    own.start()
    for p in range(A_PIECES):
        @pl.when(has_up)
        def _():
            a_copy(og.at[:, span(p, a_cols)], t, p, t + 1, a_up).start()

        @pl.when(has_dn)
        def _():
            a_copy(og.at[:, span(p, a_cols)], t, p, t - 1, a_dn).start()
    for j in range(1, nx):
        x_copy(j).start()

    def far(j, core):
        return (j - 1) * 2 + core

    def h_mate(i):
        rows_i = span(i, h_rows)
        return remote(hid_v.at[rows_i], hid_own.at[c, rows_i], hp_send.at[i], ho_recv.at[c, i], dp=mate)

    def h_own(i):
        rows_i = span(i, h_rows)
        out = []
        for j in range(1, nx):
            slot = far(nx - j, c)
            out.append(remote(
                hid_v.at[rows_i], hid_far.at[slot, rows_i], hx_send.at[j, i], hf_recv.at[slot, i],
                dp=other(j) * 2 + c,
            ))
        out.append(h_mate(i))
        out.append(pltpu.make_async_copy(hid_v.at[rows_i], hid_own.at[c, rows_i], hl_sem.at[i]))
        return out

    def h_fwd(j, i, core):
        ref = hid_far.at[far(j, core), span(i, h_rows)]
        return remote(ref, ref, hf_send.at[j, i], hf_recv.at[far(j, core), i], dp=mate)

    def hidden_step(gate_t, up_t):
        i = pl.program_id(0)
        g = gate_t[...].astype(jnp.float32)
        u = up_t[...].astype(jnp.float32)
        hid_v[span(i, h_rows), :] = (g * jax.nn.sigmoid(g) * u).astype(jnp.bfloat16)
        for copy in h_own(i):
            copy.start()

    row_spec = pl.BlockSpec((h_rows, hidden_width), lambda i: (i, 0))
    pltpu.emit_pipeline(hidden_step, grid=(H_PIECES,), in_specs=[row_spec, row_spec])(gate, up)

    @pl.loop(0, (nt - 1) * A_PIECES)
    def _(e):
        k, p = e // A_PIECES + 1, e % A_PIECES

        @pl.when(t - k >= 0)
        def _():
            a_fwd(t - k, p, t + 1, a_up).wait_recv()

            @pl.when(has_up)
            def _():
                a_fwd(t - k, p, t + 1, a_up).start()

        @pl.when(t + k < nt)
        def _():
            a_fwd(t + k, p, t - 1, a_dn).wait_recv()

            @pl.when(has_dn)
            def _():
                a_fwd(t + k, p, t - 1, a_dn).start()

    own.wait()
    for j in range(1, nx):
        xs = other(j)
        remote(xb_v.at[xs, t], xb_v.at[xs, t], x_send.at[j], x_recv.at[xs], dp=mate).wait_recv()
        for p in range(B_PIECES):
            @pl.when(has_up)
            def _():
                b_fwd(t, xs, p, t + 1, b_up).start()

            @pl.when(has_dn)
            def _():
                b_fwd(t, xs, p, t - 1, b_dn).start()

    def c_local_copy():
        return pltpu.make_async_copy(og_v.at[:, :, span(d, dev_cols)], cols_own.at[c], c_local)

    def c_mate():
        return remote(og_v.at[:, :, span(mate, dev_cols)], cols_own.at[c], c_send, c_recv, dp=mate)

    c_local_copy().start()
    c_mate().start()

    def f_local_copy(j, o):
        return pltpu.make_async_copy(
            xb_v.at[other(j), o, :, span(c, dev_cols)], cols_far.at[far(j, c), o], f_local.at[j, o]
        )

    def f_mate(j, o, core):
        return remote(
            xb_v.at[other(j), o, :, span(1 - c, dev_cols)], cols_far.at[far(j, core), o],
            f_send.at[j, o], f_recv.at[far(j, core), o], dp=mate,
        )

    def share(j, o):
        f_local_copy(j, o).start()
        f_mate(j, o, c).start()

    for j in range(1, nx):
        share(j, t)

    b_events = (nt - 1) * (nx - 1) * B_PIECES
    h_events = (nx - 1) * H_PIECES
    h_half = h_events // 2
    steps = hidden_width // tile

    def b_arrive(e, only):
        k = e // ((nx - 1) * B_PIECES) + 1
        q = e % ((nx - 1) * B_PIECES)
        j, p = q // B_PIECES + 1, q % B_PIECES
        for o, live, to, onward, sems in (
            (t - k, t - k >= 0, t + 1, has_up, b_up),
            (t + k, t + k < nt, t - 1, has_dn, b_dn),
        ):
            wanted = onward if only else jnp.logical_not(onward)

            @pl.when(jnp.logical_and(live, wanted))
            def _():
                b_fwd(o, other(j), p, to, sems).wait_recv()
                if only:
                    b_fwd(o, other(j), p, to, sems).start()

                @pl.when(p == B_PIECES - 1)
                def _():
                    share(j, o)

    def h_arrive(f):
        h_fwd(f % (nx - 1) + 1, f // (nx - 1), c).wait_recv()
        h_fwd(f % (nx - 1) + 1, f // (nx - 1), c).start()

    def grad_events(i):
        count = b_events + h_half
        per_step = -(-count // steps)
        for n in range(per_step):
            e = i * per_step + n

            @pl.when(e < b_events)
            def _():
                b_arrive(e, True)

            @pl.when(jnp.logical_and(e >= b_events, e < count))
            def _():
                h_arrive(e - b_events)

    def partial_events(i):
        count = h_events - h_half
        per_step = -(-count // steps)
        for n in range(per_step):
            e = i * per_step + n - (steps * per_step - count)

            @pl.when(e >= 0)
            def _():
                h_arrive(h_half + e)

    def grad_step(w_t, gate_t, up_t, gg_t, ug_t):
        i = pl.program_id(0)
        block = og_v[...].reshape(nt * rows, width)
        grad = lax.dot_general(
            block, w_t[...], (((1,), (1,)), ((), ())), preferred_element_type=jnp.float32
        )
        g = gate_t[...].astype(jnp.float32)
        u = up_t[...].astype(jnp.float32)
        sig = jax.nn.sigmoid(g)
        gg_t[...] = (grad * u * sig * (1.0 + g * (1.0 - sig))).astype(jnp.bfloat16)
        ug_t[...] = (grad * (g * sig)).astype(jnp.bfloat16)
        grad_events(i)

    tile_spec = pl.BlockSpec((tokens, tile), lambda i: (0, i))
    pltpu.emit_pipeline(
        grad_step,
        grid=(steps,),
        in_specs=[pl.BlockSpec((tile, width), lambda i: (i, 0)), tile_spec, tile_spec],
        out_specs=[tile_spec, tile_spec],
    )(weight, gate, up, gate_grad, up_grad)

    @pl.loop(0, H_PIECES)
    def _(i):
        h_own(i)[-1].wait()
        rows_i = span(i, h_rows)
        remote(
            hid_v.at[rows_i], hid_own.at[1 - c, rows_i], hp_send.at[i], ho_recv.at[1 - c, i], dp=mate
        ).wait_recv()

    c_local_copy().wait()
    remote(og_v.at[:, :, span(mate, dev_cols)], cols_own.at[1 - c], c_send, c_recv, dp=mate).wait_recv()

    def partial_step(h_t, c_t, out_t):
        out_t[...] = lax.dot_general(
            h_t[...].reshape(2 * tokens, tile), c_t[...].reshape(2 * tokens, dev_cols),
            (((0,), (0,)), ((), ())), preferred_element_type=jnp.float32,
        )
        partial_events(pl.program_id(0))

    pltpu.emit_pipeline(
        partial_step,
        grid=(steps,),
        in_specs=[
            pl.BlockSpec((2, tokens, tile), lambda i: (0, 0, i)),
            pl.BlockSpec((2, nt, rows, dev_cols), lambda i: (0, 0, 0, 0)),
        ],
        out_specs=[pl.BlockSpec((tile, dev_cols), lambda i: (i, 0))],
    )(hid_own, cols_own, partial)

    @pl.loop(0, b_events)
    def _(e):
        b_arrive(e, False)

    c_mate().wait_send()
    for j in range(1, nx):
        x_copy(j).wait_send()

        @pl.loop(0, nt)
        def _(o):
            f_local_copy(j, o).wait()
            f_mate(j, o, c).wait_send()
            f_mate(j, o, 1 - c).wait_recv()

    @pl.loop(0, H_PIECES)
    def _(i):
        for copy in h_own(i)[:-1]:
            copy.wait_send()
        for j in range(1, nx):
            h_fwd(j, i, c).wait_send()
            h_fwd(j, i, 1 - c).wait_recv()

    @pl.loop(0, nt)
    def _(o):
        @pl.when(jnp.logical_and(has_up, o <= t))
        def _():
            for p in range(A_PIECES):
                a_fwd(o, p, t + 1, a_up).wait_send()
            for j in range(1, nx):
                for p in range(B_PIECES):
                    b_fwd(o, other(j), p, t + 1, b_up).wait_send()

        @pl.when(jnp.logical_and(has_dn, o >= t))
        def _():
            for p in range(A_PIECES):
                a_fwd(o, p, t - 1, a_dn).wait_send()
            for j in range(1, nx):
                for p in range(B_PIECES):
                    b_fwd(o, other(j), p, t - 1, b_dn).wait_send()


def on_device(out_grad, gate_pre, up_pre, down_weight):
    nt, dp = lax.axis_size("tensor"), lax.axis_size("dp")
    nx = dp // 2
    _, rows, width = out_grad.shape
    _, tokens, hidden_width = gate_pre.shape
    tile = 256 if hidden_width % 256 == 0 else 128
    bf16 = jnp.bfloat16
    dma = pltpu.SemaphoreType.DMA
    any_spec = pl.BlockSpec(memory_space=pl.ANY)
    far = 2 * (nx - 1)
    hid_own, hid_far, cols_own, cols_far, partial, gate_grad, up_grad = pl.pallas_call(
        functools.partial(exchange, nt, nx, tile),
        out_shape=(
            jax.ShapeDtypeStruct((2, tokens, hidden_width), bf16),
            jax.ShapeDtypeStruct((far, tokens, hidden_width), bf16),
            jax.ShapeDtypeStruct((2, nt, rows, width // dp), bf16),
            jax.ShapeDtypeStruct((far, nt, rows, width // dp), bf16),
            jax.ShapeDtypeStruct((hidden_width, width // dp), jnp.float32),
            jax.ShapeDtypeStruct((tokens, hidden_width), bf16),
            jax.ShapeDtypeStruct((tokens, hidden_width), bf16),
        ),
        in_specs=[any_spec] * 4,
        out_specs=[any_spec] * 7,
        scratch_shapes=[
            pltpu.VMEM((nt, rows, width), bf16),
            pltpu.VMEM((nx, nt, rows, width // nx), bf16),
            pltpu.VMEM((tokens, hidden_width), bf16),
            dma,
            dma((nt, A_PIECES)),
            dma((nt, A_PIECES)),
            dma((nt, A_PIECES)),
            dma((nx,)),
            dma((nx,)),
            dma((nt, nx, B_PIECES)),
            dma((nt, nx, B_PIECES)),
            dma((nt, nx, B_PIECES)),
            dma((nx, H_PIECES)),
            dma((H_PIECES,)),
            dma((H_PIECES,)),
            dma((2, H_PIECES)),
            dma((far, H_PIECES)),
            dma((nx, H_PIECES)),
            dma,
            dma,
            dma,
            dma((nx, nt)),
            dma((nx, nt)),
            dma((far, nt)),
        ],
        compiler_params=pltpu.CompilerParams(
            collective_id=0, has_side_effects=True, vmem_limit_bytes=56 * 2**20
        ),
    )(out_grad[0], gate_pre[0], up_pre[0], down_weight)
    scale = 1.0 / math.sqrt(tokens * dp)
    dev_cols = width // dp
    last = hidden_width // tile - 1

    def finish(h_t, c_t, part_t, gg_in, ug_in, down_t, gg_out, ug_out, sems):
        i = pl.program_id(0)
        copies = (
            pltpu.make_async_copy(gg_in, gg_out, sems.at[0]),
            pltpu.make_async_copy(ug_in, ug_out, sems.at[1]),
        )

        @pl.when(i == 0)
        def _():
            for copy in copies:
                copy.start()

        total = part_t[...] + lax.dot_general(
            h_t[...].reshape(far * tokens, tile), c_t[...].reshape(far * tokens, dev_cols),
            (((0,), (0,)), ((), ())), preferred_element_type=jnp.float32,
        )
        down_t[...] = (total * scale).astype(bf16)

        @pl.when(i == last)
        def _():
            for copy in copies:
                copy.wait()

    down_grad, gate_grad, up_grad = pl.pallas_call(
        finish,
        grid=(last + 1,),
        out_shape=(
            jax.ShapeDtypeStruct((hidden_width, dev_cols), bf16),
            jax.ShapeDtypeStruct((tokens, hidden_width), bf16),
            jax.ShapeDtypeStruct((tokens, hidden_width), bf16),
        ),
        in_specs=[
            pl.BlockSpec((far, tokens, tile), lambda i: (0, 0, i)),
            pl.BlockSpec((far, nt, rows, dev_cols), lambda i: (0, 0, 0, 0)),
            pl.BlockSpec((tile, dev_cols), lambda i: (i, 0)),
            any_spec,
            any_spec,
        ],
        out_specs=[pl.BlockSpec((tile, dev_cols), lambda i: (i, 0)), any_spec, any_spec],
        scratch_shapes=[dma((2,))],
        compiler_params=pltpu.CompilerParams(vmem_limit_bytes=48 * 2**20),
    )(hid_far, cols_far, partial, gate_grad, up_grad)
    return (gate_grad[None], up_grad[None], down_grad)


def solution(mesh):
    return jax.shard_map(
        on_device,
        mesh=mesh,
        in_specs=(
            P("dp", ("groups", "tensor"), None),
            P("dp", "groups", "tensor"),
            P("dp", "groups", "tensor"),
            P("tensor", None),
        ),
        out_specs=(
            P("dp", "groups", "tensor"),
            P("dp", "groups", "tensor"),
            P(("groups", "tensor"), "dp"),
        ),
        check_vma=False,
    )
```

```python
import functools
import math

import jax
import jax.numpy as jnp
from jax import lax
from jax.experimental import pallas as pl
from jax.experimental.pallas import tpu as pltpu
from jax.sharding import PartitionSpec as P

A_PIECES = 4
B_PIECES = 2
H_PIECES = 8
MESH = pl.DeviceIdType.MESH


def exchange(
    nt, nx, tile,
    og, gate, up, weight,
    hid_own, hid_far, cols_own, cols_far, partial, gate_grad, up_grad,
    og_v, xb_v, hid_v,
    own_sem, a_recv, a_up, a_dn, x_send, x_recv, b_recv, b_up, b_dn,
    hx_send, hp_send, hl_sem, ho_recv, hf_recv, hf_send,
    c_local, c_send, c_recv, f_local, f_send, f_recv,
):
    t = lax.axis_index("tensor")
    d = lax.axis_index("dp")
    x, c = d // 2, d % 2
    mate = x * 2 + (1 - c)
    rows, width = og.shape
    tokens, hidden_width = gate.shape
    chip_cols = width // nx
    dev_cols = width // (2 * nx)
    a_cols = width // A_PIECES
    b_cols = chip_cols // B_PIECES
    h_rows = tokens // H_PIECES
    has_up, has_dn = t < nt - 1, t > 0

    def span(i, size):
        return pl.ds(pl.multiple_of(i * size, size), size)

    def remote(src, dst, send, recv, **where):
        return pltpu.make_async_remote_copy(
            src_ref=src, dst_ref=dst, send_sem=send, recv_sem=recv,
            device_id=where, device_id_type=MESH,
        )

    def other(j):
        return (x + j) % nx

    barrier = pltpu.get_barrier_semaphore()

    @pl.when(has_up)
    def _():
        pl.semaphore_signal(barrier, 1, device_id={"tensor": t + 1}, device_id_type=MESH)

    @pl.when(has_dn)
    def _():
        pl.semaphore_signal(barrier, 1, device_id={"tensor": t - 1}, device_id_type=MESH)

    pl.semaphore_signal(barrier, 1, device_id={"dp": mate}, device_id_type=MESH)
    for j in range(1, nx):
        pl.semaphore_signal(barrier, 1, device_id={"dp": other(j) * 2 + c}, device_id_type=MESH)
    inner = jnp.logical_and(has_up, has_dn)

    @pl.when(inner)
    def _():
        pl.semaphore_wait(barrier, nx + 2)

    @pl.when(jnp.logical_not(inner))
    def _():
        pl.semaphore_wait(barrier, nx + 1)

    def a_copy(src, o, p, to, sems):
        return remote(src, og_v.at[o, :, span(p, a_cols)], sems.at[o, p], a_recv.at[o, p], tensor=to)

    def a_fwd(o, p, to, sems):
        return a_copy(og_v.at[o, :, span(p, a_cols)], o, p, to, sems)

    def b_fwd(o, xs, p, to, sems):
        ref = xb_v.at[xs, o, :, span(p, b_cols)]
        return remote(ref, ref, sems.at[o, xs, p], b_recv.at[o, xs, p], tensor=to)

    def x_copy(j):
        xo = other(j)
        return remote(
            og.at[:, span(xo, chip_cols)], xb_v.at[x, t], x_send.at[j], x_recv.at[x], dp=xo * 2 + c
        )

    own = pltpu.make_async_copy(og, og_v.at[t], own_sem)
    own.start()
    for p in range(A_PIECES):
        @pl.when(has_up)
        def _():
            a_copy(og.at[:, span(p, a_cols)], t, p, t + 1, a_up).start()

        @pl.when(has_dn)
        def _():
            a_copy(og.at[:, span(p, a_cols)], t, p, t - 1, a_dn).start()
    for j in range(1, nx):
        x_copy(j).start()

    def far(j, core):
        return (j - 1) * 2 + core

    def h_mate(i):
        rows_i = span(i, h_rows)
        return remote(hid_v.at[rows_i], hid_own.at[c, rows_i], hp_send.at[i], ho_recv.at[c, i], dp=mate)

    def h_own(i):
        rows_i = span(i, h_rows)
        out = []
        for j in range(1, nx):
            slot = far(nx - j, c)
            out.append(remote(
                hid_v.at[rows_i], hid_far.at[slot, rows_i], hx_send.at[j, i], hf_recv.at[slot, i],
                dp=other(j) * 2 + c,
            ))
        out.append(h_mate(i))
        out.append(pltpu.make_async_copy(hid_v.at[rows_i], hid_own.at[c, rows_i], hl_sem.at[i]))
        return out

    def h_fwd(j, i, core):
        ref = hid_far.at[far(j, core), span(i, h_rows)]
        return remote(ref, ref, hf_send.at[j, i], hf_recv.at[far(j, core), i], dp=mate)

    def hidden_step(gate_t, up_t):
        i = pl.program_id(0)
        g = gate_t[...].astype(jnp.float32)
        u = up_t[...].astype(jnp.float32)
        hid_v[span(i, h_rows), :] = (g * jax.nn.sigmoid(g) * u).astype(jnp.bfloat16)
        for copy in h_own(i):
            copy.start()

    row_spec = pl.BlockSpec((h_rows, hidden_width), lambda i: (i, 0))
    pltpu.emit_pipeline(hidden_step, grid=(H_PIECES,), in_specs=[row_spec, row_spec])(gate, up)

    @pl.loop(0, (nt - 1) * A_PIECES)
    def _(e):
        k, p = e // A_PIECES + 1, e % A_PIECES

        @pl.when(t - k >= 0)
        def _():
            a_fwd(t - k, p, t + 1, a_up).wait_recv()

            @pl.when(has_up)
            def _():
                a_fwd(t - k, p, t + 1, a_up).start()

        @pl.when(t + k < nt)
        def _():
            a_fwd(t + k, p, t - 1, a_dn).wait_recv()

            @pl.when(has_dn)
            def _():
                a_fwd(t + k, p, t - 1, a_dn).start()

    own.wait()
    for j in range(1, nx):
        xs = other(j)
        remote(xb_v.at[xs, t], xb_v.at[xs, t], x_send.at[j], x_recv.at[xs], dp=mate).wait_recv()
        for p in range(B_PIECES):
            @pl.when(has_up)
            def _():
                b_fwd(t, xs, p, t + 1, b_up).start()

            @pl.when(has_dn)
            def _():
                b_fwd(t, xs, p, t - 1, b_dn).start()

    def c_local_copy():
        return pltpu.make_async_copy(og_v.at[:, :, span(d, dev_cols)], cols_own.at[c], c_local)

    def c_mate():
        return remote(og_v.at[:, :, span(mate, dev_cols)], cols_own.at[c], c_send, c_recv, dp=mate)

    c_local_copy().start()
    c_mate().start()

    def f_local_copy(j, o):
        return pltpu.make_async_copy(
            xb_v.at[other(j), o, :, span(c, dev_cols)], cols_far.at[far(j, c), o], f_local.at[j, o]
        )

    def f_mate(j, o, core):
        return remote(
            xb_v.at[other(j), o, :, span(1 - c, dev_cols)], cols_far.at[far(j, core), o],
            f_send.at[j, o], f_recv.at[far(j, core), o], dp=mate,
        )

    def share(j, o):
        f_local_copy(j, o).start()
        f_mate(j, o, c).start()

    for j in range(1, nx):
        share(j, t)

    b_events = (nt - 1) * (nx - 1) * B_PIECES
    h_events = (nx - 1) * H_PIECES
    h_half = h_events // 2
    steps = hidden_width // tile

    def b_arrive(e, only):
        k = e // ((nx - 1) * B_PIECES) + 1
        q = e % ((nx - 1) * B_PIECES)
        j, p = q // B_PIECES + 1, q % B_PIECES
        for o, live, to, onward, sems in (
            (t - k, t - k >= 0, t + 1, has_up, b_up),
            (t + k, t + k < nt, t - 1, has_dn, b_dn),
        ):
            wanted = onward if only else jnp.logical_not(onward)

            @pl.when(jnp.logical_and(live, wanted))
            def _():
                b_fwd(o, other(j), p, to, sems).wait_recv()
                if only:
                    b_fwd(o, other(j), p, to, sems).start()

                @pl.when(p == B_PIECES - 1)
                def _():
                    share(j, o)

    def h_arrive(f):
        h_fwd(f % (nx - 1) + 1, f // (nx - 1), c).wait_recv()
        h_fwd(f % (nx - 1) + 1, f // (nx - 1), c).start()

    def grad_events(i):
        count = b_events + h_half
        per_step = -(-count // steps)
        for n in range(per_step):
            e = i * per_step + n

            @pl.when(e < b_events)
            def _():
                b_arrive(e, True)

            @pl.when(jnp.logical_and(e >= b_events, e < count))
            def _():
                h_arrive(e - b_events)

    def partial_events(i):
        count = h_events - h_half
        per_step = -(-count // steps)
        for n in range(per_step):
            e = i * per_step + n - (steps * per_step - count)

            @pl.when(e >= 0)
            def _():
                h_arrive(h_half + e)

    def grad_step(w_t, gate_t, up_t, gg_t, ug_t):
        i = pl.program_id(0)
        block = og_v[...].reshape(nt * rows, width)
        grad = lax.dot_general(
            block, w_t[...], (((1,), (1,)), ((), ())), preferred_element_type=jnp.float32
        )
        g = gate_t[...].astype(jnp.float32)
        u = up_t[...].astype(jnp.float32)
        sig = jax.nn.sigmoid(g)
        gg_t[...] = (grad * u * sig * (1.0 + g * (1.0 - sig))).astype(jnp.bfloat16)
        ug_t[...] = (grad * (g * sig)).astype(jnp.bfloat16)
        grad_events(i)

    tile_spec = pl.BlockSpec((tokens, tile), lambda i: (0, i))
    pltpu.emit_pipeline(
        grad_step,
        grid=(steps,),
        in_specs=[pl.BlockSpec((tile, width), lambda i: (i, 0)), tile_spec, tile_spec],
        out_specs=[tile_spec, tile_spec],
    )(weight, gate, up, gate_grad, up_grad)

    @pl.loop(0, H_PIECES)
    def _(i):
        h_own(i)[-1].wait()
        rows_i = span(i, h_rows)
        remote(
            hid_v.at[rows_i], hid_own.at[1 - c, rows_i], hp_send.at[i], ho_recv.at[1 - c, i], dp=mate
        ).wait_recv()

    c_local_copy().wait()
    remote(og_v.at[:, :, span(mate, dev_cols)], cols_own.at[1 - c], c_send, c_recv, dp=mate).wait_recv()

    def partial_step(h_t, c_t, out_t):
        out_t[...] = lax.dot_general(
            h_t[...].reshape(2 * tokens, tile), c_t[...].reshape(2 * tokens, dev_cols),
            (((0,), (0,)), ((), ())), preferred_element_type=jnp.float32,
        ).astype(jnp.bfloat16)
        partial_events(pl.program_id(0))

    pltpu.emit_pipeline(
        partial_step,
        grid=(steps,),
        in_specs=[
            pl.BlockSpec((2, tokens, tile), lambda i: (0, 0, i)),
            pl.BlockSpec((2, nt, rows, dev_cols), lambda i: (0, 0, 0, 0)),
        ],
        out_specs=[pl.BlockSpec((tile, dev_cols), lambda i: (i, 0))],
    )(hid_own, cols_own, partial)

    @pl.loop(0, b_events)
    def _(e):
        b_arrive(e, False)

    c_mate().wait_send()
    for j in range(1, nx):
        x_copy(j).wait_send()

        @pl.loop(0, nt)
        def _(o):
            f_local_copy(j, o).wait()
            f_mate(j, o, c).wait_send()
            f_mate(j, o, 1 - c).wait_recv()

    @pl.loop(0, H_PIECES)
    def _(i):
        for copy in h_own(i)[:-1]:
            copy.wait_send()
        for j in range(1, nx):
            h_fwd(j, i, c).wait_send()
            h_fwd(j, i, 1 - c).wait_recv()

    @pl.loop(0, nt)
    def _(o):
        @pl.when(jnp.logical_and(has_up, o <= t))
        def _():
            for p in range(A_PIECES):
                a_fwd(o, p, t + 1, a_up).wait_send()
            for j in range(1, nx):
                for p in range(B_PIECES):
                    b_fwd(o, other(j), p, t + 1, b_up).wait_send()

        @pl.when(jnp.logical_and(has_dn, o >= t))
        def _():
            for p in range(A_PIECES):
                a_fwd(o, p, t - 1, a_dn).wait_send()
            for j in range(1, nx):
                for p in range(B_PIECES):
                    b_fwd(o, other(j), p, t - 1, b_dn).wait_send()


def on_device(out_grad, gate_pre, up_pre, down_weight):
    nt, dp = lax.axis_size("tensor"), lax.axis_size("dp")
    nx = dp // 2
    _, rows, width = out_grad.shape
    _, tokens, hidden_width = gate_pre.shape
    tile = 256 if hidden_width % 256 == 0 else 128
    bf16 = jnp.bfloat16
    dma = pltpu.SemaphoreType.DMA
    any_spec = pl.BlockSpec(memory_space=pl.ANY)
    far = 2 * (nx - 1)
    hid_own, hid_far, cols_own, cols_far, partial, gate_grad, up_grad = pl.pallas_call(
        functools.partial(exchange, nt, nx, tile),
        out_shape=(
            jax.ShapeDtypeStruct((2, tokens, hidden_width), bf16),
            jax.ShapeDtypeStruct((far, tokens, hidden_width), bf16),
            jax.ShapeDtypeStruct((2, nt, rows, width // dp), bf16),
            jax.ShapeDtypeStruct((far, nt, rows, width // dp), bf16),
            jax.ShapeDtypeStruct((hidden_width, width // dp), bf16),
            jax.ShapeDtypeStruct((tokens, hidden_width), bf16),
            jax.ShapeDtypeStruct((tokens, hidden_width), bf16),
        ),
        in_specs=[any_spec] * 4,
        out_specs=[any_spec] * 7,
        scratch_shapes=[
            pltpu.VMEM((nt, rows, width), bf16),
            pltpu.VMEM((nx, nt, rows, width // nx), bf16),
            pltpu.VMEM((tokens, hidden_width), bf16),
            dma,
            dma((nt, A_PIECES)),
            dma((nt, A_PIECES)),
            dma((nt, A_PIECES)),
            dma((nx,)),
            dma((nx,)),
            dma((nt, nx, B_PIECES)),
            dma((nt, nx, B_PIECES)),
            dma((nt, nx, B_PIECES)),
            dma((nx, H_PIECES)),
            dma((H_PIECES,)),
            dma((H_PIECES,)),
            dma((2, H_PIECES)),
            dma((far, H_PIECES)),
            dma((nx, H_PIECES)),
            dma,
            dma,
            dma,
            dma((nx, nt)),
            dma((nx, nt)),
            dma((far, nt)),
        ],
        compiler_params=pltpu.CompilerParams(
            collective_id=0, has_side_effects=True, vmem_limit_bytes=56 * 2**20
        ),
    )(out_grad[0], gate_pre[0], up_pre[0], down_weight)
    scale = 1.0 / math.sqrt(tokens * dp)
    total = partial.astype(jnp.float32) + jnp.einsum(
        "tf,td->fd",
        hid_far.reshape(far * tokens, hidden_width),
        cols_far.reshape(far * tokens, width // dp),
        preferred_element_type=jnp.float32,
    )
    down_grad = (total * scale).astype(bf16)
    return (gate_grad[None], up_grad[None], down_grad)


def solution(mesh):
    return jax.shard_map(
        on_device,
        mesh=mesh,
        in_specs=(
            P("dp", ("groups", "tensor"), None),
            P("dp", "groups", "tensor"),
            P("dp", "groups", "tensor"),
            P("tensor", None),
        ),
        out_specs=(
            P("dp", "groups", "tensor"),
            P("dp", "groups", "tensor"),
            P(("groups", "tensor"), "dp"),
        ),
        check_vma=False,
    )
```
